128 devices in a mesh: section: 4 (over x), tensor: 32 (over z, y, core).
Axes of the slice: x: 4, y: 4, z: 4, core: 2. Of those that a mesh axis runs over, the one named last changes fastest.
Arguments:
- inputs: bfloat16 [4, 1024, 8192], P('section', None, 'tensor'), may hold values from -6 to 6
- preact: bfloat16 [4, 1024, 32768], P('section', None, 'tensor'), may hold values from -6 to 6
- handoff: bfloat16 [4, 1024, 8192], P('section', None, 'tensor'), may hold values from -6 to 6
- first_blocks: bfloat16 [4, 128, 6, 256, 256], P('section', 'tensor'), may hold values from -0.15625 to 0.15625
- second_blocks: bfloat16 [4, 128, 6, 256, 256], P('section', 'tensor'), may hold values from -0.078125 to 0.078125
- left_one: bfloat16 [4, 8192, 256], P('section', 'tensor'), may hold values from -0.0625 to 0.0625
- right_one: bfloat16 [4, 256, 32768], P('section', None, 'tensor'), may hold values from -0.375 to 0.375
- left_two: bfloat16 [4, 32768, 256], P('section', 'tensor'), may hold values from -0.03125 to 0.03125
- right_two: bfloat16 [4, 256, 8192], P('section', None, 'tensor'), may hold values from -0.375 to 0.375
Outputs:
- input_grad: bfloat16 [4, 1024, 8192], P('section', None, 'tensor')
- first_grad: bfloat16 [4, 128, 6, 256, 256], P('section', 'tensor')
- second_grad: bfloat16 [4, 128, 6, 256, 256], P('section', 'tensor')
- leftone_grad: bfloat16 [4, 8192, 256], P('section', 'tensor')
- rightone_grad: bfloat16 [4, 256, 32768], P('section', None, 'tensor')
- lefttwo_grad: bfloat16 [4, 32768, 256], P('section', 'tensor')
- righttwo_grad: bfloat16 [4, 256, 8192], P('section', None, 'tensor')
The draws below stay inside these ranges and needn't reach their ends.
All inputs are finite; a program needn't handle non-finite values.
Results may differ from the reference program's by a relative error of at most 0.0061.
Values may be sent and summed in bfloat16 or wider, within the bound.
A program may use at most 128 MiB of HBM per device.

```python
import jax
import jax.numpy as jnp
import numpy as np

D = 8192
FF = 32768
BLOCK = 256
RANK = 256
LEVELS = 5
TOKENS = 1024
SECTIONS = 4
LINKS = 6
IN_BLOCKS = 32
HID_BLOCKS = 128
GROUP = 4


def steps_of(rng, dims, pieces, smallest, largest):
    gain, own = 1.0, jax.random.fold_in(rng, 6)
    for dim, blocks in pieces:
        heights = jnp.exp(jax.random.uniform(jax.random.fold_in(own, dim), (blocks,), jnp.float32, smallest / len(pieces), largest / len(pieces)))
        gain = gain * jnp.repeat(heights, dims[dim] // blocks).reshape([-1 if axis == dim else 1 for axis in range(len(dims))])
    return gain


def bell_draw(key, shape, scale, reach, pieces=(), kind=jnp.bfloat16):
    array = scale * jax.random.normal(key, shape, jnp.float32)
    if pieces:
        array = array * steps_of(key, shape, pieces, -0.22, 0.18)
    return jnp.clip(array, -reach, reach).astype(kind)


def setup_inputs(seed: int = 0) -> dict:
    arg_keys = jax.random.split(jax.random.key(seed), 10)
    return {
        "inputs": bell_draw(arg_keys[0], (SECTIONS, TOKENS, D), 1.0, 6.0, ((0, 4), (2, 32))),
        "preact": bell_draw(arg_keys[1], (SECTIONS, TOKENS, FF), 1.0, 6.0, ((0, 4), (2, 32))),
        "handoff": bell_draw(arg_keys[2], (SECTIONS, TOKENS, D), 1.0, 6.0, ((0, 4), (2, 32))),
        "first_blocks": bell_draw(arg_keys[3], (SECTIONS, HID_BLOCKS, LINKS, BLOCK, BLOCK), (LINKS * BLOCK) ** -0.5, 0.15625, ((0, 4), (1, 32))),
        "second_blocks": bell_draw(arg_keys[4], (SECTIONS, HID_BLOCKS, LINKS, BLOCK, BLOCK), (LINKS * GROUP * BLOCK) ** -0.5, 0.078125, ((0, 4), (1, 32))),
        "left_one": bell_draw(arg_keys[5], (SECTIONS, D, RANK), D ** -0.5, 0.0625, ((0, 4), (1, 32))),
        "right_one": bell_draw(arg_keys[6], (SECTIONS, RANK, FF), RANK ** -0.5, 0.375, ((0, 4), (2, 32))),
        "left_two": bell_draw(arg_keys[7], (SECTIONS, FF, RANK), FF ** -0.5, 0.03125, ((0, 4), (1, 32))),
        "right_two": bell_draw(arg_keys[8], (SECTIONS, RANK, D), RANK ** -0.5, 0.375, ((0, 4), (2, 32))),
    }


def gelu_pair(preact):
    values = preact.astype(jnp.float32)
    normal_cdf = 0.5 * (1.0 + jax.scipy.special.erf(values * 0.7071067811865476))
    density = jnp.exp(-0.5 * values * values) * 0.3989422804014327
    return values * normal_cdf, normal_cdf + values * density


def partner_table(count_in, degree):
    if degree == 0:
        return np.arange(count_in)
    return np.arange(count_in) ^ (1 << (degree - 1))


def one_section(inputs, preact, upstream, first_blocks, second_blocks, left_one, right_one, left_two, right_two):
    token_count = inputs.shape[0]
    link_count = LEVELS + 1
    home_block = np.arange(HID_BLOCKS) // GROUP
    activated, slope_vals = gelu_pair(preact)
    activated = activated.astype(jnp.bfloat16)
    proj_in = jnp.dot(inputs, left_one, preferred_element_type=jnp.float32).astype(jnp.bfloat16)
    proj_act = jnp.dot(activated, left_two, preferred_element_type=jnp.float32).astype(jnp.bfloat16)
    proj_grad = jnp.dot(upstream, right_two.T, preferred_element_type=jnp.float32).astype(jnp.bfloat16)
    grad_act = jnp.dot(proj_grad, left_two.T, preferred_element_type=jnp.float32).reshape(token_count, HID_BLOCKS, BLOCK)
    up_blocks = upstream.astype(jnp.float32).reshape(token_count, IN_BLOCKS, BLOCK)
    in_blocks = inputs.astype(jnp.float32).reshape(token_count, IN_BLOCKS, BLOCK)
    for degree in range(link_count):
        link_table = partner_table(IN_BLOCKS, degree)[home_block]
        grad_act = grad_act + jnp.einsum('tib,ieb->tie', up_blocks[:, link_table], second_blocks[:, degree].astype(jnp.float32))
    hidden_grad = (grad_act.reshape(token_count, FF) * slope_vals).astype(jnp.bfloat16)
    back_rank = jnp.dot(hidden_grad, right_one.T, preferred_element_type=jnp.float32).astype(jnp.bfloat16)
    hid_blocks = hidden_grad.astype(jnp.float32).reshape(token_count, HID_BLOCKS, BLOCK)
    act_blocks = activated.astype(jnp.float32).reshape(token_count, HID_BLOCKS, BLOCK)
    summed_grad = jnp.dot(back_rank, left_one.T, preferred_element_type=jnp.float32).reshape(token_count, IN_BLOCKS, BLOCK)
    first_list = []
    second_list = []
    for degree in range(link_count):
        partner = partner_table(IN_BLOCKS, degree)
        link_table = partner[home_block]
        partial_value = jnp.einsum('tie,ibe->tib', hid_blocks, first_blocks[:, degree].astype(jnp.float32))
        grouped = partial_value.reshape(token_count, IN_BLOCKS, GROUP, BLOCK).sum(axis=2)
        summed_grad = summed_grad + grouped[:, partner]
        first_list.append(jnp.einsum('tib,tie->ibe', in_blocks[:, link_table], hid_blocks).astype(jnp.bfloat16))
        second_list.append(jnp.einsum('tie,tib->ieb', act_blocks, up_blocks[:, link_table]).astype(jnp.bfloat16))
    input_grad = summed_grad.reshape(token_count, D).astype(jnp.bfloat16)
    first_grad = jnp.stack(first_list, axis=1)
    second_grad = jnp.stack(second_list, axis=1)
    leftone_grad = jnp.dot(inputs.T, back_rank, preferred_element_type=jnp.float32).astype(jnp.bfloat16)
    rightone_grad = jnp.dot(proj_in.T, hidden_grad, preferred_element_type=jnp.float32).astype(jnp.bfloat16)
    lefttwo_grad = jnp.dot(activated.T, proj_grad, preferred_element_type=jnp.float32).astype(jnp.bfloat16)
    righttwo_grad = jnp.dot(proj_act.T, upstream, preferred_element_type=jnp.float32).astype(jnp.bfloat16)
    return (input_grad, first_grad, second_grad, leftone_grad, rightone_grad, lefttwo_grad, righttwo_grad)


def reference(inputs, preact, handoff, first_blocks, second_blocks, left_one, right_one, left_two, right_two):
    collected = []
    for section_pos in range(SECTIONS):
        collected.append(one_section(inputs[section_pos], preact[section_pos], handoff[(section_pos + 1) % SECTIONS],
                                   first_blocks[section_pos], second_blocks[section_pos], left_one[section_pos],
                                   right_one[section_pos], left_two[section_pos], right_two[section_pos]))
    stacked = [jnp.stack([member[number] for member in collected]) for number in range(7)]
    return (stacked[0], stacked[1], stacked[2], stacked[3], stacked[4], stacked[5], stacked[6])
```

```python
import jax
import jax.numpy as jnp
from jax import lax
from jax.sharding import PartitionSpec as P


def swapped(value, axis, apart):
    mask = 2**apart
    pairs = [(source, source ^ mask) for source in range(lax.axis_size(axis))]
    return lax.ppermute(value, axis, pairs)


def shifted(shard, axis, by):
    peers = lax.axis_size(axis)
    return lax.ppermute(shard, axis, [(i, (i + by) % peers) for i in range(peers)])


def summed(values):
    part = lax.psum_scatter(values, "tensor", scatter_dimension=0, tiled=True)
    return lax.all_gather(part.astype(jnp.bfloat16), "tensor", axis=0, tiled=True)


def gelu_pair(preact):
    values = preact.astype(jnp.float32)
    normal_cdf = 0.5 * (1.0 + jax.scipy.special.erf(values * 0.7071067811865476))
    density = jnp.exp(-0.5 * values * values) * 0.3989422804014327
    return (values * normal_cdf, normal_cdf + values * density)


def partner_sets(values, count_in, link_count, swapper):
    local_bits = count_in.bit_length() - 1
    result = [values]
    for degree in range(1, link_count):
        result.append(swapper(values, degree - 1 - local_bits))
    return result


def body(
    inputs, preact, handoff, first_blocks, second_blocks, left_one, right_one, left_two, right_two
):
    own_inputs = inputs[0]
    blocks_one = first_blocks[0]
    blocks_two = second_blocks[0]
    hid_count = blocks_one.shape[0]
    link_count = blocks_one.shape[1]
    block_size = blocks_one.shape[-1]
    row_count = own_inputs.shape[0]
    feat_width = own_inputs.shape[1]
    count_in = feat_width // block_size
    group_size = hid_count // count_in
    local_bits = count_in.bit_length() - 1
    activated, slope_vals = gelu_pair(preact[0])
    activated = activated.astype(jnp.bfloat16)
    proj_in = summed(jnp.dot(own_inputs, left_one[0], preferred_element_type=jnp.float32))
    proj_act = summed(jnp.dot(activated, left_two[0], preferred_element_type=jnp.float32))

    def swap_inputs(values, bit_pos):
        return swapped(values, "tensor", bit_pos)

    def swap_grads(values, bit_pos):
        return swapped(values, "tensor", bit_pos)

    input_sets = jnp.stack(partner_sets(own_inputs, count_in, link_count, swap_inputs))
    upstream = shifted(handoff[0], "section", -1)
    grad_sets = jnp.stack(partner_sets(upstream, count_in, link_count, swap_grads))
    proj_grad = summed(jnp.dot(upstream, right_two[0].T, preferred_element_type=jnp.float32))
    grad_view = grad_sets.reshape(link_count, row_count, count_in, block_size)
    second_view = blocks_two.reshape(count_in, group_size, link_count, block_size, block_size)
    grad_act = jnp.einsum(
        "ktcb,cjkeb->tcje", grad_view, second_view, preferred_element_type=jnp.float32
    ).reshape(row_count, hid_count * block_size)
    grad_act = grad_act + jnp.dot(proj_grad, left_two[0].T, preferred_element_type=jnp.float32)
    hidden_grad = (grad_act * slope_vals).astype(jnp.bfloat16)
    back_rank = summed(jnp.dot(hidden_grad, right_one[0].T, preferred_element_type=jnp.float32))
    hidden_view = hidden_grad.reshape(row_count, count_in, group_size, block_size)
    first_view = blocks_one.reshape(count_in, group_size, link_count, block_size, block_size)
    partials = jnp.einsum(
        "tcje,cjkbe->ktcb", hidden_view, first_view, preferred_element_type=jnp.float32
    ).reshape(link_count, row_count, feat_width)
    summed_grad = partials[0] + jnp.dot(
        back_rank, left_one[0].T, preferred_element_type=jnp.float32
    )
    degree_order = list(range(1, link_count))
    for degree in degree_order:
        summed_grad = summed_grad + swapped(partials[degree], "tensor", degree - 1 - local_bits)
    input_grad = summed_grad.astype(jnp.bfloat16)[None]
    input_view = input_sets.reshape(link_count, row_count, count_in, block_size)
    first_grad = jnp.einsum(
        "ktcb,tcje->cjkbe", input_view, hidden_view, preferred_element_type=jnp.float32
    )
    first_grad = first_grad.reshape(hid_count, link_count, block_size, block_size).astype(
        jnp.bfloat16
    )[None]
    activ_view = activated.reshape(row_count, count_in, group_size, block_size)
    second_grad = jnp.einsum(
        "tcje,ktcb->cjkeb", activ_view, grad_view, preferred_element_type=jnp.float32
    )
    second_grad = second_grad.reshape(hid_count, link_count, block_size, block_size).astype(
        jnp.bfloat16
    )[None]
    leftone_grad = jnp.dot(own_inputs.T, back_rank, preferred_element_type=jnp.float32).astype(
        jnp.bfloat16
    )[None]
    rightone_grad = jnp.dot(proj_in.T, hidden_grad, preferred_element_type=jnp.float32).astype(
        jnp.bfloat16
    )[None]
    lefttwo_grad = jnp.dot(activated.T, proj_grad, preferred_element_type=jnp.float32).astype(
        jnp.bfloat16
    )[None]
    righttwo_grad = jnp.dot(proj_act.T, upstream, preferred_element_type=jnp.float32).astype(
        jnp.bfloat16
    )[None]
    return (
        input_grad,
        first_grad,
        second_grad,
        leftone_grad,
        rightone_grad,
        lefttwo_grad,
        righttwo_grad,
    )


def solution(mesh):
    in_specs = (
        P("section", None, "tensor"),
        P("section", None, "tensor"),
        P("section", None, "tensor"),
        P("section", "tensor", None, None, None),
        P("section", "tensor", None, None, None),
        P("section", "tensor", None),
        P("section", None, "tensor"),
        P("section", "tensor", None),
        P("section", None, "tensor"),
    )
    out_specs = (
        P("section", None, "tensor"),
        P("section", "tensor", None, None, None),
        P("section", "tensor", None, None, None),
        P("section", "tensor", None),
        P("section", None, "tensor"),
        P("section", "tensor", None),
        P("section", None, "tensor"),
    )
    return jax.shard_map(body, mesh=mesh, in_specs=in_specs, out_specs=out_specs, check_vma=False)
```

```python
import itertools

import jax
import jax.numpy as jnp
from jax import lax
from jax.experimental import pallas as pl
from jax.experimental.pallas import tpu as pltpu
from jax.sharding import PartitionSpec as P

MESH = pl.DeviceIdType.MESH
F32 = jnp.float32
BF16 = jnp.bfloat16
NT = (((1,), (1,)), ((), ()))
CHUNKS = 4
MASKS = {"c": (1,), "y": (2, 4, 6), "z": (8, 16, 24)}


def nt(a, b):
    return lax.dot_general(a, b, NT, preferred_element_type=F32)


def nn(a, b):
    return jnp.dot(a, b, preferred_element_type=F32)


def at(start, size):
    return pl.ds(pl.multiple_of(start, size), size)


def flipped(index, mask):
    result = index
    for bit in range(5):
        if mask >> bit & 1:
            weight = 1 << bit
            result = result + weight * (1 - 2 * ((index // weight) % 2))
    return result


def kernel(
    x_h, pre_h, hand_h, fb_h, sb_h, l1_h, r1_h, l2_h, r2_h,
    ig_o, fg_o, sg_o, l1_o, r1_o, l2_o, r2_o,
    xin, xt, u, act, act_t, slope, ga, w1, w2, hid, l1, r2, paf, br,
    p_out, p_in, sg, fg, ig, l1g, r1g, l2g, r2g,
    pg_ar, pa_ar, br_ar, ssem, rsem, lsem,
):
    tokens = xin.shape[0]
    width = tokens // CHUNKS
    me = lax.axis_index("tensor")
    sec = lax.axis_index("section")
    core, row, col = me % 2, (me // 2) % 4, me // 8
    place = {"c": core, "y": row, "z": col}
    step_of = {"c": 1, "y": 2, "z": 8}
    peer = {m: {"tensor": flipped(me, m)} for m in (1, 2, 4, 6, 8, 16, 24)}
    before, after = {"section": (sec + 3) % 4}, {"section": (sec + 1) % 4}
    numbers, locals_ = itertools.count(), itertools.count()
    sends, stores = [], []

    def send(src, dst, to):
        n = next(numbers)
        copy = pltpu.make_async_remote_copy(
            src_ref=src, dst_ref=dst, send_sem=ssem.at[n], recv_sem=rsem.at[n],
            device_id=to, device_id_type=MESH,
        )
        copy.start()
        sends.append(copy)
        return copy

    def local(src, dst):
        copy = pltpu.make_async_copy(src, dst, lsem.at[next(locals_)])
        copy.start()
        return copy

    def rows(c):
        return pl.ds(c * width, width)

    in_x = local(x_h, xin)
    in_pre = [local(pre_h.at[rows(c)], act.at[rows(c)]) for c in range(CHUNKS)]
    in_small = [local(l1_h, l1), local(r2_h, r2), local(l2_h, w2.at[6])]
    in_w2 = [local(sb_h.at[i], w2.at[pl.ds(0, 6), pl.ds(i * 256, 256)]) for i in range(4)]
    in_w1 = [local(fb_h.at[i], w1.at[pl.ds(0, 6), :, pl.ds(i * 256, 256)]) for i in range(4)]
    in_w1.append(local(r1_h, w1.at[6]))

    barrier = pltpu.get_barrier_semaphore()
    greeted = [*peer.values(), before, after]
    for to in greeted:
        pl.semaphore_signal(barrier, inc=1, device_id=to, device_id_type=MESH)
    pl.semaphore_wait(barrier, len(greeted))

    up0 = [send(hand_h.at[rows(c)], u.at[0, rows(c)], before) for c in range(CHUNKS)]

    in_x.wait()
    halves = [pl.ds(h * 128, 128) for h in range(2)]
    x1, x2, x4, x3, x5 = [], [], [], [], []
    for h in halves:
        xt[0, h, :] = xin[:, h].T
        x2.append(send(xt.at[0, h], xt.at[2, h], peer[2]))
        x4.append(send(xt.at[0, h], xt.at[4, h], peer[8]))
        x1.append(send(xt.at[0, h], xt.at[1, h], peer[1]))

    def pass_inputs(n):
        x2[n].wait_recv()
        x3.append(send(xt.at[2, halves[n]], xt.at[3, halves[n]], peer[6]))
        x4[n].wait_recv()
        x5.append(send(xt.at[4, halves[n]], xt.at[5, halves[n]], peer[24]))

    def summing(bufs, total, order):
        part, part_b, got1, s1, s1_b, got2, s2, s2_b, got3 = bufs
        size = part.shape[0]
        half, quarter, piece = size // 2, size // 8, size // 32
        second, third = order
        base1 = core * half
        base2 = base1 + place[second] * quarter
        base3 = base2 + place[third] * piece

        other = (1 - core) * half
        copy = send(part_b.at[at(other, half)], got1, peer[1])
        yield
        copy.wait_recv()
        s1[...] = part[at(base1, half), :] + got1[...].astype(F32)
        s1_b[...] = s1[...].astype(BF16)
        copies = []
        for n, m in enumerate(MASKS[second]):
            spot = (flipped(me, m) // step_of[second]) % 4
            copies.append(send(s1_b.at[at(spot * quarter, quarter)], got2.at[n], peer[m]))
        yield
        for copy in copies:
            copy.wait_recv()
        mine = s1[at(place[second] * quarter, quarter), :]
        s2[...] = mine + got2[0].astype(F32) + got2[1].astype(F32) + got2[2].astype(F32)
        s2_b[...] = s2[...].astype(BF16)
        copies = []
        for n, m in enumerate(MASKS[third]):
            spot = (flipped(me, m) // step_of[third]) % 4
            copies.append(send(s2_b.at[at(spot * piece, piece)], got3.at[n], peer[m]))
        yield
        for copy in copies:
            copy.wait_recv()
        mine = s2[at(place[third] * piece, piece), :]
        whole = mine + got3[0].astype(F32) + got3[1].astype(F32) + got3[2].astype(F32)
        spot = at(base3, piece)
        total[spot, :] = whole.astype(BF16)
        copies = [send(total.at[spot], total.at[spot], peer[m]) for m in MASKS[third]]
        yield
        for copy in copies:
            copy.wait_recv()
        spot = at(base2, quarter)
        copies = [send(total.at[spot], total.at[spot], peer[m]) for m in MASKS[second]]
        yield
        for copy in copies:
            copy.wait_recv()
        spot = at(base1, half)
        copy = send(total.at[spot], total.at[spot], peer[1])
        yield
        copy.wait_recv()
        yield

    for copy in in_small:
        copy.wait()
    up1, up2, up3, up4, up5 = [], [], [], [], []

    def pass_upstream(c):
        up2[c].wait_recv()
        up3.append(send(u.at[2, rows(c)], u.at[3, rows(c)], peer[6]))
        up4[c].wait_recv()
        up5.append(send(u.at[4, rows(c)], u.at[5, rows(c)], peer[24]))

    for c in range(CHUNKS):
        in_pre[c].wait()

        @pl.loop(0, width // 32)
        def _(r):
            spot = pl.ds(pl.multiple_of(c * width + r * 32, 32), 32)
            for j in range(4):
                lanes = pl.ds(j * 256, 256)
                v = act[spot, lanes].astype(F32)
                cdf = 0.5 * (1.0 + lax.erf(v * 0.7071067811865476))
                density = jnp.exp(-0.5 * v * v) * 0.3989422804014327
                act[spot, lanes] = (v * cdf).astype(BF16)
                slope[spot, lanes] = cdf + v * density

        up0[c].wait_recv()
        up2.append(send(u.at[0, rows(c)], u.at[2, rows(c)], peer[2]))
        up4.append(send(u.at[0, rows(c)], u.at[4, rows(c)], peer[8]))
        up1.append(send(u.at[0, rows(c)], u.at[1, rows(c)], peer[1]))
        value = nt(u[0, rows(c), :], r2[...])
        pg_ar[0][rows(c), :] = value
        pg_ar[1][rows(c), :] = value.astype(BF16)
        if c >= 1:
            pass_upstream(c - 1)
        if c in (1, 2):
            pass_inputs(c - 1)

        @pl.loop(0, 4)
        def _(j):
            act_t[at(j * 256, 256), rows(c)] = act[rows(c), at(j * 256, 256)].T

    pg = summing(pg_ar, u.at[6], ("y", "z"))
    next(pg)
    pass_upstream(CHUNKS - 1)

    left = l1[...].T
    pa_ar[0][pl.ds(0, 256), :] = nn(left, xt[0])
    left = w2[6].T
    pa_ar[0][pl.ds(256, 256), :] = nn(left, act_t[...])
    pa_ar[1][...] = pa_ar[0][...].astype(BF16)
    next(pg)
    pa = summing(pa_ar, paf, ("z", "y"))
    next(pa)

    for copy in in_w2:
        copy.wait()

    def block_terms(c):
        for group in (up1, up2, up3, up4, up5):
            if group is not up2 and group is not up4:
                group[c].wait_recv()
        left = jnp.concatenate([u[k, rows(c), :] for k in range(6)], axis=1)

        @pl.loop(0, 4)
        def _(j):
            block = at(j * 256, 256)
            right = jnp.concatenate([w2[k, block, :] for k in range(6)], axis=1)
            ga[rows(c), block] = nt(left, right)

    def second_terms(first, last):
        @pl.loop(first, last)
        def _(k):
            value = nn(act_t[...], u[k]).astype(BF16)
            for i in range(4):
                sg[i, k] = value[i * 256 : (i + 1) * 256]

    block_terms(0)
    next(pg)
    block_terms(1)
    next(pa)
    block_terms(2)
    next(pg)
    block_terms(3)
    next(pa)
    second_terms(0, 1)
    next(pg)
    second_terms(1, 2)
    next(pa)
    next(pg)
    second_terms(2, 4)
    next(pa)
    next(pg)

    for copy in in_w1:
        copy.wait()
    in1, in2, in4, got2, got4 = [], [], [], [], []

    def merge(c):
        got2[c].wait_recv()
        p_out[1, rows(c), :] = (ga[rows(c), pl.ds(256, 256)] + p_in[3, rows(c), :].astype(F32)).astype(BF16)
        in2.append(send(p_out.at[1, rows(c)], p_in.at[1, rows(c)], peer[2]))
        got4[c].wait_recv()
        p_out[2, rows(c), :] = (ga[rows(c), pl.ds(512, 256)] + p_in[4, rows(c), :].astype(F32)).astype(BF16)
        in4.append(send(p_out.at[2, rows(c)], p_in.at[2, rows(c)], peer[8]))

    for c in range(CHUNKS):

        @pl.loop(0, 4)
        def _(j):
            block = at(j * 256, 256)
            grad = ga[rows(c), block] + nt(u[6, rows(c), :], w2[6, block, :])
            hid[rows(c), block] = (grad * slope[rows(c), block]).astype(BF16)

        h = hid[rows(c), :]
        p_out[3, rows(c), :] = nt(h, w1[3]).astype(BF16)
        got2.append(send(p_out.at[3, rows(c)], p_in.at[3, rows(c)], peer[6]))
        p_out[4, rows(c), :] = nt(h, w1[5]).astype(BF16)
        got4.append(send(p_out.at[4, rows(c)], p_in.at[4, rows(c)], peer[24]))
        p_out[0, rows(c), :] = nt(h, w1[1]).astype(BF16)
        in1.append(send(p_out.at[0, rows(c)], p_in.at[0, rows(c)], peer[1]))
        value = nt(h, w1[6])
        br_ar[0][rows(c), :] = value
        br_ar[1][rows(c), :] = value.astype(BF16)
        ga[rows(c), pl.ds(256, 256)] = nt(h, w1[2])
        ga[rows(c), pl.ds(512, 256)] = nt(h, w1[4])
        ga[rows(c), pl.ds(0, 256)] = nt(h, w1[0])
        if c >= 1:
            merge(c - 1)

    back = summing(br_ar, br, ("y", "z"))
    next(back)
    next(pa)
    second_terms(4, 6)
    stores.append(local(sg, sg_o))
    merge(CHUNKS - 1)
    next(back)
    next(pa)
    for group in (x1, x3, x5):
        for copy in group:
            copy.wait_recv()

    def first_terms(first, last):
        @pl.loop(first, last)
        def _(k):
            for i in range(4):
                block = pl.ds(i * 256, 256)
                fg[i, k] = nn(xt[k], hid[:, block]).astype(BF16)

    first_terms(0, 2)
    next(back)
    first_terms(2, 4)
    next(back)
    first_terms(4, 6)
    stores.append(local(fg, fg_o))
    next(back)
    l2g[...] = nn(act_t[...], u[6]).astype(BF16)
    stores.append(local(l2g, l2_o))
    r1g[...] = nn(paf[pl.ds(0, 256), :], hid[...]).astype(BF16)
    stores.append(local(r1g, r1_o))
    next(back)
    r2g[...] = nn(paf[pl.ds(256, 256), :], u[0]).astype(BF16)
    stores.append(local(r2g, r2_o))
    next(back)
    l1g[...] = nn(xt[0], br[...]).astype(BF16)
    stores.append(local(l1g, l1_o))
    for c in range(CHUNKS):
        value = ga[rows(c), pl.ds(0, 256)] + nt(br[rows(c), :], l1[...])
        for n, group in enumerate((in1, in2, in4)):
            group[c].wait_recv()
            value = value + p_in[n, rows(c), :].astype(F32)
        ig[rows(c), :] = value.astype(BF16)
        stores.append(local(ig.at[rows(c)], ig_o.at[rows(c)]))
    for copy in sends:
        copy.wait_send()
    for copy in stores:
        copy.wait()


def sum_buffers(size, lanes):
    return (
        pltpu.VMEM((size, lanes), F32),
        pltpu.VMEM((size, lanes), BF16),
        pltpu.VMEM((size // 2, lanes), BF16),
        pltpu.VMEM((size // 2, lanes), F32),
        pltpu.VMEM((size // 2, lanes), BF16),
        pltpu.VMEM((3, size // 8, lanes), BF16),
        pltpu.VMEM((size // 8, lanes), F32),
        pltpu.VMEM((size // 8, lanes), BF16),
        pltpu.VMEM((3, size // 32, lanes), BF16),
    )


def body(*args):
    args = [a[0] for a in args]
    x, pre, _, fb, _, l1, r1, l2, r2 = args
    t, b = x.shape
    h = pre.shape[1]
    k = fb.shape[1]
    outs = [x, fb, fb, l1, r1, l2, r2]
    vm = pltpu.VMEM
    scratch = [
        vm((t, b), BF16), vm((k, b, t), BF16), vm((k + 1, t, b), BF16), vm((t, h), BF16),
        vm((h, t), BF16), vm((t, h), F32), vm((t, h), F32), vm((k + 1, b, h), BF16),
        vm((k + 1, h, b), BF16), vm((t, h), BF16), vm((b, b), BF16), vm((b, b), BF16),
        vm((2 * b, t), BF16), vm((t, b), BF16), vm((5, t, b), BF16), vm((5, t, b), BF16),
        vm(fb.shape, BF16), vm(fb.shape, BF16), vm((t, b), BF16), vm((b, b), BF16),
        vm((b, h), BF16), vm((h, b), BF16), vm((b, b), BF16),
        sum_buffers(t, b), sum_buffers(2 * b, t), sum_buffers(t, b),
        pltpu.SemaphoreType.DMA((112,)), pltpu.SemaphoreType.DMA((112,)),
        pltpu.SemaphoreType.DMA((40,)),
    ]
    results = pl.pallas_call(
        kernel,
        out_shape=[jax.ShapeDtypeStruct(o.shape, o.dtype) for o in outs],
        in_specs=[pl.BlockSpec(memory_space=pl.ANY)] * 9,
        out_specs=[pl.BlockSpec(memory_space=pl.ANY)] * 7,
        scratch_shapes=scratch,
        compiler_params=pltpu.CompilerParams(
            collective_id=0, has_side_effects=True, vmem_limit_bytes=62 * 1024 * 1024
        ),
    )(*args)
    return tuple(r[None] for r in results)


def solution(mesh):
    three = P("section", None, "tensor")
    rows = P("section", "tensor", None)
    blocks = P("section", "tensor", None, None, None)
    return jax.shard_map(
        body,
        mesh=mesh,
        in_specs=(three, three, three, blocks, blocks, rows, three, rows, three),
        out_specs=(three, blocks, blocks, rows, three, rows, three),
        check_vma=False,
    )
```

```python
import itertools

import jax
import jax.numpy as jnp
from jax import lax
from jax.experimental import pallas as pl
from jax.experimental.pallas import tpu as pltpu
from jax.sharding import PartitionSpec as P

MESH = pl.DeviceIdType.MESH
F32 = jnp.float32
BF16 = jnp.bfloat16
NT = (((1,), (1,)), ((), ()))
CHUNKS = 4
MASKS = {"c": (1,), "y": (2, 4, 6), "z": (8, 16, 24)}


def nt(a, b):
    return lax.dot_general(a, b, NT, preferred_element_type=F32)


def nn(a, b):
    return jnp.dot(a, b, preferred_element_type=F32)


def at(start, size):
    return pl.ds(pl.multiple_of(start, size), size)


def flipped(index, mask):
    result = index
    for bit in range(5):
        if mask >> bit & 1:
            weight = 1 << bit
            result = result + weight * (1 - 2 * ((index // weight) % 2))
    return result


def kernel(
    x_h, pre_h, hand_h, fb_h, sb_h, l1_h, r1_h, l2_h, r2_h,
    ig, fg, sg, l1g, r1g, l2g, r2g,
    xin, hand, xt, u, act, act_t, slope, ga, w1, w2, hid, l1, r2, paf, br,
    p_out, p_in, pg_ar, pa_ar, br_ar, ssem, rsem, lsem,
):
    tokens = xin.shape[0]
    width = tokens // CHUNKS
    me = lax.axis_index("tensor")
    sec = lax.axis_index("section")
    core, row, col = me % 2, (me // 2) % 4, me // 8
    peer = {m: {"tensor": flipped(me, m)} for m in (1, 2, 4, 6, 8, 16, 24)}
    before, after = {"section": (sec + 3) % 4}, {"section": (sec + 1) % 4}
    numbers, locals_ = itertools.count(), itertools.count()

    taken = {}

    def spot_of(kind, key):
        return taken.setdefault((kind, key), sum(k == kind for k, _ in taken))

    def send(src, dst, to, name, arrival=None):
        count = next(numbers)
        copy = pltpu.make_async_remote_copy(
            src_ref=src,
            dst_ref=dst,
            send_sem=ssem.at[spot_of("send", name)],
            recv_sem=rsem.at[spot_of("recv", arrival or count)],
            device_id=to,
            device_id_type=MESH,
        )
        copy.start()
        return copy

    def sent(name, ref):
        pltpu.make_async_copy(ref, ref, ssem.at[taken["send", name]]).wait()

    def got(name, ref):
        pltpu.make_async_copy(ref, ref, rsem.at[taken["recv", name]]).wait()

    def local(src, dst, name=None):
        copy = pltpu.make_async_copy(src, dst, lsem.at[spot_of("local", name or next(locals_))])
        copy.start()
        return copy

    def loaded(name, ref):
        pltpu.make_async_copy(ref, ref, lsem.at[taken["local", name]]).wait()

    def rows(c):
        return pl.ds(c * width, width)

    in_hand = local(hand_h, hand)
    in_x = local(x_h, xin)
    in_pre = [local(pre_h.at[rows(c)], act.at[rows(c)]) for c in range(CHUNKS)]
    in_small = [local(l1_h, l1), local(l2_h, w2.at[6])]
    for i in range(4):
        local(sb_h.at[i], w2.at[pl.ds(0, 6), pl.ds(i * 256, 256)], "w2")
    for i in range(4):
        local(fb_h.at[i], w1.at[pl.ds(0, 6), :, pl.ds(i * 256, 256)], "w1")
    local(r1_h, w1.at[6], "w1")

    barrier = pltpu.get_barrier_semaphore()
    greeted = [{"tensor": flipped(me, m)} for m in (1, *range(2, 32, 2))] + [before, after]
    for to in greeted:
        pl.semaphore_signal(barrier, inc=1, device_id=to, device_id_type=MESH)
    pl.semaphore_wait(barrier, len(greeted))

    in_r2 = send(r2_h, r2, after, "r2")
    up0 = [send(hand_h.at[rows(c)], u.at[0, rows(c)], before, "hand") for c in range(CHUNKS)]

    def mixed(a, b):
        return a * (1 - core) + b * core

    flips_y = [flipped(me, m) for m in MASKS["y"]]
    flips_z = [flipped(me, m) for m in MASKS["z"]]
    second_to = [{"tensor": mixed(a, b)} for a, b in zip(flips_y, flips_z)]
    third_to = [{"tensor": mixed(b, a)} for a, b in zip(flips_y, flips_z)]
    second_at = [mixed((a // 2) % 4, b // 8) for a, b in zip(flips_y, flips_z)]
    third_at = [mixed(b // 8, (a // 2) % 4) for a, b in zip(flips_y, flips_z)]
    second_me, third_me = mixed(row, col), mixed(col, row)

    def summing(bufs, total, name):
        part, got1, s1, s1_b, got2, s2, got3, _ = bufs
        size = part.shape[0]
        half, quarter, piece = size // 2, size // 8, size // 32
        base1 = core * half
        base2 = base1 + second_me * quarter
        base3 = base2 + third_me * piece

        send(part.at[at((1 - core) * half, half)], got1, peer[1], name + "1", name + "1")
        yield
        got(name + "1", got1)
        s1[...] = part[at(core * half, half), :] + got1[...]
        s1_b[...] = s1[...].astype(BF16)
        for n in range(3):
            spot = at(second_at[n] * quarter, quarter)
            send(s1_b.at[spot], got2.at[n], second_to[n], name + "2", name + "2")
        yield
        got(name + "2", got2)
        mine = s1[at(second_me * quarter, quarter), :]
        s2[...] = mine + got2[0].astype(F32) + got2[1].astype(F32) + got2[2].astype(F32)
        for n in range(3):
            spot = at(third_at[n] * piece, piece)
            send(s2.at[spot], got3.at[n], third_to[n], name + "3", name + "3")
        yield
        got(name + "3", got3)
        mine = s2[at(third_me * piece, piece), :]
        spot = at(base3, piece)
        total[spot, :] = (mine + got3[0] + got3[1] + got3[2]).astype(BF16)
        for to in third_to:
            send(total.at[spot], total.at[spot], to, name + "4", name + "4")
        yield
        got(name + "4", s1_b.at[pl.ds(0, 3 * piece)])
        spot = at(base2, quarter)
        for to in second_to:
            send(total.at[spot], total.at[spot], to, name + "5", name + "5")
        yield
        got(name + "5", got2)
        spot = at(base1, half)
        send(total.at[spot], total.at[spot], peer[1], name + "6", name + "6")
        yield
        got(name + "6", s1_b)
        yield

    others = [flipped(me, m) for m in range(2, 32, 2)]

    def summing_all(bufs, total, name, ship=False):
        part, got1, s1, s1_b, got2, shipped = bufs
        size = part.shape[0]
        half, piece = size // 2, size // 32
        mine = core * half + (me // 2) * piece

        send(part.at[at((1 - core) * half, half)], got1, peer[1], name + "1", name + "1")
        yield
        got(name + "1", got1)
        s1[...] = part[at(core * half, half), :] + got1[...]
        s1_b[...] = s1[...].astype(BF16)
        for n, to in enumerate(others):
            spot = at((to // 2) * piece, piece)
            send(s1_b.at[spot], got2.at[n], {"tensor": to}, name + "2", name + "2")
        yield
        got(name + "2", got2)
        whole = s1[at((me // 2) * piece, piece), :]
        for n in range(len(others)):
            whole = whole + got2[n].astype(F32)
        spot = at(mine, piece)
        if ship:
            shipped[...] = whole.astype(BF16)
            send(shipped, total.at[spot], before, name + "3", name + "3")
            yield
            got(name + "3", shipped)
        else:
            total[spot, :] = whole.astype(BF16)
        for to in others:
            send(total.at[spot], total.at[spot], {"tensor": to}, name + "4", name + "4")
        yield
        got(name + "4", got2)
        spot = at(core * half, half)
        send(total.at[spot], total.at[spot], peer[1], name + "5", name + "5")
        yield
        got(name + "5", s1_b)
        yield

    def activate(c):
        in_pre[c].wait()

        @pl.loop(0, width // 32)
        def _(r):
            spot = pl.ds(pl.multiple_of(c * width + r * 32, 32), 32)
            for j in range(4):
                lanes = pl.ds(j * 256, 256)
                v = act[spot, lanes].astype(F32)
                cdf = 0.5 * (1.0 + lax.erf(v * 0.7071067811865476))
                density = jnp.exp(-0.5 * v * v) * 0.3989422804014327
                act[spot, lanes] = (v * cdf).astype(BF16)
                slope[spot, lanes] = cdf + v * density

        @pl.loop(0, 4)
        def _(j):
            act_t[at(j * 256, 256), rows(c)] = act[rows(c), at(j * 256, 256)].T

    up2, up3, up4, up5 = [], [], [], []

    def give_upstream(c):
        up0[c].wait_recv()
        up2.append(send(u.at[0, rows(c)], u.at[2, rows(c)], peer[2], "up"))
        up4.append(send(u.at[0, rows(c)], u.at[4, rows(c)], peer[8], "up"))
        send(u.at[0, rows(c)], u.at[1, rows(c)], peer[1], "up", "up1")

    def pass_upstream(c):
        up2[c].wait_recv()
        up3.append(send(u.at[2, rows(c)], u.at[3, rows(c)], peer[6], "up"))
        up4[c].wait_recv()
        up5.append(send(u.at[4, rows(c)], u.at[5, rows(c)], peer[24], "up"))

    x2, x4 = [], []
    parts = [pl.ds(n * 64, 64) for n in range(4)]

    def give_inputs(n):
        x2.append(send(xt.at[0, parts[n]], xt.at[2, parts[n]], peer[2], "in"))
        x4.append(send(xt.at[0, parts[n]], xt.at[4, parts[n]], peer[8], "in"))
        send(xt.at[0, parts[n]], xt.at[1, parts[n]], peer[1], "in", "in")

    def pass_inputs(n):
        x2[n].wait_recv()
        send(xt.at[2, parts[n]], xt.at[3, parts[n]], peer[6], "in", "in")
        x4[n].wait_recv()
        send(xt.at[4, parts[n]], xt.at[5, parts[n]], peer[24], "in", "in")

    def block_terms(c):
        for group in (up3, up5):
            group[c].wait_recv()
        left = jnp.concatenate([u[k, rows(c), :] for k in range(6)], axis=1)

        @pl.loop(0, 4)
        def _(j):
            block = at(j * 256, 256)
            right = jnp.concatenate([w2[k, block, :] for k in range(6)], axis=1)
            ga[rows(c), block] = nt(left, right)

    def second_terms(first, last):
        @pl.loop(first, last)
        def _(k):
            value = nn(act_t[...], u[k]).astype(BF16)
            for i in range(4):
                sg[i, k] = value[i * 256 : (i + 1) * 256]

    in_x.wait()
    for n in range(2):
        xt[0, pl.ds(n * 128, 128), :] = xin[:, pl.ds(n * 128, 128)].T
    give_inputs(0)
    give_inputs(1)
    activate(0)
    activate(1)
    activate(2)
    in_hand.wait()
    in_r2.wait_recv()
    pg_ar[0][...] = nt(hand[...], r2[...])
    pg = summing_all(pg_ar, u.at[6], "pg", ship=True)
    next(pg)
    give_upstream(0)
    activate(3)
    next(pg)
    pass_inputs(0)
    for copy in in_small:
        copy.wait()
    pa_ar[0][pl.ds(0, 256), :] = nn(l1[...].T, xt[0])
    pa_ar[0][pl.ds(256, 256), :] = nn(w2[6].T, act_t[...])
    pa = summing(pa_ar, paf, "pa")
    next(pa)
    give_upstream(1)
    pass_inputs(1)
    pass_upstream(0)
    give_upstream(2)
    give_upstream(3)
    pass_upstream(1)
    second_terms(0, 1)
    give_inputs(2)
    pass_upstream(2)
    next(pg)
    got("up1", u.at[1])
    second_terms(1, 2)
    pass_upstream(3)
    next(pg)
    next(pa)
    give_inputs(3)
    loaded("w2", w2.at[pl.ds(0, 6)])
    block_terms(0)
    block_terms(1)
    pass_inputs(2)
    second_terms(2, 3)
    block_terms(2)
    second_terms(4, 5)
    block_terms(3)
    next(pg)
    second_terms(3, 4)
    pass_inputs(3)
    second_terms(5, 6)
    next(pg)
    next(pa)

    loaded("w1", w1)
    far2, far4 = [], []

    def hidden(c):
        @pl.loop(0, 2)
        def _(j):
            block = at(j * 512, 512)
            grad = ga[rows(c), block] + nt(u[6, rows(c), :], w2[6, block, :])
            hid[rows(c), block] = (grad * slope[rows(c), block]).astype(BF16)

    def both(h):
        return pl.ds(h * 2 * width, 2 * width)

    def far_terms(h):
        p_out[3, both(h), :] = nt(hid[both(h), :], w1[3]).astype(BF16)
        p_out[4, both(h), :] = nt(hid[both(h), :], w1[5]).astype(BF16)

    def far_sends(h):
        for c in (2 * h, 2 * h + 1):
            far2.append(send(p_out.at[3, rows(c)], p_in.at[3, rows(c)], peer[6], "p"))
            far4.append(send(p_out.at[4, rows(c)], p_in.at[4, rows(c)], peer[24], "p"))

    def near_terms(h):
        left = hid[both(h), :]
        p_out[0, both(h), :] = nt(left, w1[1]).astype(BF16)
        for c in (2 * h, 2 * h + 1):
            send(p_out.at[0, rows(c)], p_in.at[0, rows(c)], peer[1], "p", "p")
        ga[both(h), pl.ds(256, 256)] = nt(left, w1[2])
        ga[both(h), pl.ds(512, 256)] = nt(left, w1[4])
        ga[both(h), pl.ds(0, 256)] = nt(left, w1[0])

    def merge(c):
        for n, far, mask in ((1, far2, 2), (2, far4, 8)):
            far[c].wait_recv()
            own = ga[rows(c), pl.ds(256 * n, 256)]
            p_out[n, rows(c), :] = (own + p_in[n + 2, rows(c), :].astype(F32)).astype(BF16)
            send(p_out.at[n, rows(c)], p_in.at[n, rows(c)], peer[mask], "p", "p")

    def first_terms(first, last):
        @pl.loop(first, last)
        def _(k):
            for i in range(4):
                block = pl.ds(i * 256, 256)
                fg[i, k] = nn(xt[k], hid[:, block]).astype(BF16)

    for c in range(CHUNKS):
        hidden(c)
    br_ar[0][...] = nt(hid[...], w1[6])
    back = summing_all(br_ar, br, "br")
    next(back)
    next(pa)
    far_terms(0)
    next(back)
    next(pa)
    far_sends(0)
    near_terms(0)
    far_terms(1)
    far_sends(1)
    near_terms(1)
    got("in", xt.at[pl.ds(0, 3)])
    first_terms(0, 2)
    merge(0)
    next(back)
    first_terms(2, 3)
    merge(1)
    first_terms(3, 4)
    next(pa)
    merge(2)
    first_terms(4, 5)
    merge(3)
    first_terms(5, 6)
    l2g[...] = nn(act_t[...], u[6]).astype(BF16)
    next(back)
    next(pa)
    r1g[...] = nn(paf[pl.ds(0, 256), :], hid[...]).astype(BF16)
    r2g[...] = nn(paf[pl.ds(256, 256), :], u[0]).astype(BF16)
    got("p", p_in.at[pl.ds(0, 3)])
    for c in range(CHUNKS):
        value = ga[rows(c), pl.ds(0, 256)]
        for n in range(3):
            value = value + p_in[n, rows(c), :].astype(F32)
        ga[rows(c), pl.ds(0, 256)] = value
    next(back)
    l1g[...] = nn(xt[0], br[...]).astype(BF16)
    ig[...] = (ga[:, pl.ds(0, 256)] + nt(br[...], l1[...])).astype(BF16)
    sent("r2", r2)
    sent("hand", hand)
    sent("up", u.at[pl.ds(0, 5)])
    sent("in", xt.at[pl.ds(0, 5)])
    sent("p", p_out)
    for name, (part, got1, s1, s1_b, got2, *_) in (("pg", pg_ar), ("br", br_ar)):
        sent(name + "1", got1)
        sent(name + "2", got2)
        if name == "pg":
            sent("pg3", pg_ar[5])
        sent(name + "4", got2)
        sent(name + "5", s1_b)
    part, got1, s1, s1_b, got2, s2, got3, _ = pa_ar
    sent("pa1", got1)
    sent("pa2", got2)
    sent("pa3", got3)
    sent("pa4", s1_b.at[pl.ds(0, 48)])
    sent("pa5", got2)
    sent("pa6", s1_b)


def write_out(*refs):
    count = len(refs) // 2
    sems = refs[-1]
    copies = [pltpu.make_async_copy(refs[n], refs[count + n], sems.at[n]) for n in range(count)]
    for copy in copies:
        copy.start()
    for copy in copies:
        copy.wait()


def sum_buffers(size, lanes):
    return (
        pltpu.VMEM((size, lanes), F32),
        pltpu.VMEM((size // 2, lanes), F32),
        pltpu.VMEM((size // 2, lanes), F32),
        pltpu.VMEM((size // 2, lanes), BF16),
        pltpu.VMEM((3, size // 8, lanes), BF16),
        pltpu.VMEM((size // 8, lanes), F32),
        pltpu.VMEM((3, size // 32, lanes), F32),
        pltpu.VMEM((size // 32, lanes), BF16),
    )


def wide_buffers(size, lanes):
    return (
        pltpu.VMEM((size, lanes), F32),
        pltpu.VMEM((size // 2, lanes), F32),
        pltpu.VMEM((size // 2, lanes), F32),
        pltpu.VMEM((size // 2, lanes), BF16),
        pltpu.VMEM((15, size // 32, lanes), BF16),
        pltpu.VMEM((size // 32, lanes), BF16),
    )


def body(*args):
    args = [a[0] for a in args]
    x, pre, _, fb, _, l1, r1, l2, r2 = args
    t, b = x.shape
    h = pre.shape[1]
    k = fb.shape[1]
    outs = [x, fb, fb, l1, r1, l2, r2]
    vm = pltpu.VMEM
    scratch = [
        vm((t, b), BF16), vm((t, b), BF16), vm((k, b, t), BF16), vm((k + 1, t, b), BF16),
        vm((t, h), BF16), vm((h, t), BF16), vm((t, h), F32), vm((t, h), F32),
        vm((k + 1, b, h), BF16), vm((k + 1, h, b), BF16), vm((t, h), BF16), vm((b, b), BF16),
        vm((b, b), BF16), vm((2 * b, t), BF16), vm((t, b), BF16), vm((5, t, b), BF16),
        vm((5, t, b), BF16), wide_buffers(t, b), sum_buffers(2 * b, t),
        wide_buffers(t, b),
        pltpu.SemaphoreType.DMA((20,)), pltpu.SemaphoreType.DMA((55,)),
        pltpu.SemaphoreType.DMA((11,)),
    ]
    results = pl.pallas_call(
        kernel,
        out_shape=[pltpu.VMEM(o.shape, o.dtype) for o in outs],
        in_specs=[pl.BlockSpec(memory_space=pl.ANY)] * 9,
        out_specs=[pl.BlockSpec(memory_space=pltpu.VMEM)] * 7,
        scratch_shapes=scratch,
        compiler_params=pltpu.CompilerParams(
            collective_id=0, has_side_effects=True, vmem_limit_bytes=50 * 1024 * 1024
        ),
    )(*args)
    results = pl.pallas_call(
        write_out,
        out_shape=[jax.ShapeDtypeStruct(o.shape, o.dtype) for o in outs],
        in_specs=[pl.BlockSpec(memory_space=pltpu.VMEM)] * 7,
        out_specs=[pl.BlockSpec(memory_space=pl.ANY)] * 7,
        scratch_shapes=[pltpu.SemaphoreType.DMA((7,))],
        compiler_params=pltpu.CompilerParams(vmem_limit_bytes=2 * 1024 * 1024),
    )(*[pltpu.with_memory_space_constraint(r, pltpu.VMEM) for r in results])
    return tuple(r[None] for r in results)


def solution(mesh):
    three = P("section", None, "tensor")
    rows = P("section", "tensor", None)
    blocks = P("section", "tensor", None, None, None)
    return jax.shard_map(
        body,
        mesh=mesh,
        in_specs=(three, three, three, blocks, blocks, rows, three, rows, three),
        out_specs=(three, blocks, blocks, rows, three, rows, three),
        check_vma=False,
    )
```

```python
import itertools

import jax
import jax.numpy as jnp
from jax import lax
from jax.experimental import pallas as pl
from jax.experimental.pallas import tpu as pltpu
from jax.sharding import PartitionSpec as P

MESH = pl.DeviceIdType.MESH
F32 = jnp.float32
BF16 = jnp.bfloat16
NT = (((1,), (1,)), ((), ()))
CHUNKS = 4
MASKS = {"c": (1,), "y": (2, 4, 6), "z": (8, 16, 24)}


def nt(a, b):
    return lax.dot_general(a, b, NT, preferred_element_type=F32)


def nn(a, b):
    return jnp.dot(a, b, preferred_element_type=F32)


def at(start, size):
    return pl.ds(pl.multiple_of(start, size), size)


def flipped(index, mask):
    result = index
    for bit in range(5):
        if mask >> bit & 1:
            weight = 1 << bit
            result = result + weight * (1 - 2 * ((index // weight) % 2))
    return result


def kernel(
    x_h, pre_h, hand_h, fb_h, sb_h, l1_h, r1_h, l2_h, r2_h,
    ig, fg, sg, l1g, r1g, l2g, r2g,
    xin, hand, xt, u, act, act_t, slope, ga, w1, w2, hid, l1, r2, paf, br,
    p_out, p_in, pg_ar, pa_ar, br_ar, ssem, rsem, lsem,
):
    tokens = xin.shape[0]
    width = tokens // CHUNKS
    me = lax.axis_index("tensor")
    sec = lax.axis_index("section")
    core, row, col = me % 2, (me // 2) % 4, me // 8
    peer = {m: {"tensor": flipped(me, m)} for m in (1, 2, 4, 6, 8, 16, 24)}
    before, after = {"section": (sec + 3) % 4}, {"section": (sec + 1) % 4}
    numbers, locals_ = itertools.count(), itertools.count()

    taken = {}

    def spot_of(kind, key):
        return taken.setdefault((kind, key), sum(k == kind for k, _ in taken))

    def send(src, dst, to, name, arrival=None):
        count = next(numbers)
        copy = pltpu.make_async_remote_copy(
            src_ref=src,
            dst_ref=dst,
            send_sem=ssem.at[spot_of("send", name)],
            recv_sem=rsem.at[spot_of("recv", arrival or count)],
            device_id=to,
            device_id_type=MESH,
        )
        copy.start()
        return copy

    def sent(name, ref):
        pltpu.make_async_copy(ref, ref, ssem.at[taken["send", name]]).wait()

    def got(name, ref):
        pltpu.make_async_copy(ref, ref, rsem.at[taken["recv", name]]).wait()

    def local(src, dst, name=None):
        copy = pltpu.make_async_copy(src, dst, lsem.at[spot_of("local", name or next(locals_))])
        copy.start()
        return copy

    def loaded(name, ref):
        pltpu.make_async_copy(ref, ref, lsem.at[taken["local", name]]).wait()

    def rows(c):
        return pl.ds(c * width, width)

    in_hand = local(hand_h, hand)
    in_x = local(x_h, xin)
    in_pre = [local(pre_h.at[rows(c)], act.at[rows(c)]) for c in range(CHUNKS)]
    in_small = [local(l1_h, l1), local(l2_h, w2.at[6])]
    for i in range(4):
        local(sb_h.at[i], w2.at[pl.ds(0, 6), pl.ds(i * 256, 256)], "w2")
    for i in range(4):
        local(fb_h.at[i], w1.at[pl.ds(0, 6), :, pl.ds(i * 256, 256)], "w1")
    local(r1_h, w1.at[6], "w1")

    barrier = pltpu.get_barrier_semaphore()
    greeted = [{"tensor": flipped(me, m)} for m in (1, *range(2, 32, 2))] + [before, after]
    for to in greeted:
        pl.semaphore_signal(barrier, inc=1, device_id=to, device_id_type=MESH)
    pl.semaphore_wait(barrier, len(greeted))

    in_r2 = send(r2_h, r2, after, "r2")
    up0 = [send(hand_h.at[rows(c)], u.at[0, rows(c)], before, "hand") for c in range(CHUNKS)]

    def mixed(a, b):
        return a * (1 - core) + b * core

    flips_y = [flipped(me, m) for m in MASKS["y"]]
    flips_z = [flipped(me, m) for m in MASKS["z"]]
    second_to = [{"tensor": mixed(a, b)} for a, b in zip(flips_y, flips_z)]
    third_to = [{"tensor": mixed(b, a)} for a, b in zip(flips_y, flips_z)]
    second_at = [mixed((a // 2) % 4, b // 8) for a, b in zip(flips_y, flips_z)]
    third_at = [mixed(b // 8, (a // 2) % 4) for a, b in zip(flips_y, flips_z)]
    second_me, third_me = mixed(row, col), mixed(col, row)

    def summing(bufs, total, name):
        part, got1, s1, s1_b, got2, s2, got3, _ = bufs
        size = part.shape[0]
        half, quarter, piece = size // 2, size // 8, size // 32
        base1 = core * half
        base2 = base1 + second_me * quarter
        base3 = base2 + third_me * piece

        send(part.at[at((1 - core) * half, half)], got1, peer[1], name + "1", name + "1")
        yield
        got(name + "1", got1)
        s1[...] = part[at(core * half, half), :] + got1[...]
        s1_b[...] = s1[...].astype(BF16)
        for n in range(3):
            spot = at(second_at[n] * quarter, quarter)
            send(s1_b.at[spot], got2.at[n], second_to[n], name + "2", name + "2")
        yield
        got(name + "2", got2)
        mine = s1[at(second_me * quarter, quarter), :]
        s2[...] = mine + got2[0].astype(F32) + got2[1].astype(F32) + got2[2].astype(F32)
        for n in range(3):
            spot = at(third_at[n] * piece, piece)
            send(s2.at[spot], got3.at[n], third_to[n], name + "3", name + "3")
        yield
        got(name + "3", got3)
        mine = s2[at(third_me * piece, piece), :]
        spot = at(base3, piece)
        total[spot, :] = (mine + got3[0] + got3[1] + got3[2]).astype(BF16)
        for to in third_to:
            send(total.at[spot], total.at[spot], to, name + "4", name + "4")
        yield
        got(name + "4", s1_b.at[pl.ds(0, 3 * piece)])
        spot = at(base2, quarter)
        for to in second_to:
            send(total.at[spot], total.at[spot], to, name + "5", name + "5")
        yield
        got(name + "5", got2)
        spot = at(base1, half)
        send(total.at[spot], total.at[spot], peer[1], name + "6", name + "6")
        yield
        got(name + "6", s1_b)
        yield

    others = [flipped(me, m) for m in range(2, 32, 2)]

    def summing_all(bufs, total, name, ship=False):
        part, got1, s1, s1_b, got2, shipped = bufs
        size = part.shape[0]
        half, piece = size // 2, size // 32
        mine = core * half + (me // 2) * piece

        send(part.at[at((1 - core) * half, half)], got1, peer[1], name + "1", name + "1")
        yield
        got(name + "1", got1)
        s1[...] = part[at(core * half, half), :] + got1[...]
        s1_b[...] = s1[...].astype(BF16)
        for n, to in enumerate(others):
            spot = at((to // 2) * piece, piece)
            send(s1_b.at[spot], got2.at[n], {"tensor": to}, name + "2", name + "2")
        yield
        got(name + "2", got2)
        whole = s1[at((me // 2) * piece, piece), :]
        for n in range(len(others)):
            whole = whole + got2[n].astype(F32)
        spot = at(mine, piece)
        if ship:
            shipped[...] = whole.astype(BF16)
            send(shipped, total.at[spot], before, name + "3", name + "3")
            yield
            got(name + "3", shipped)
        else:
            total[spot, :] = whole.astype(BF16)
        for to in others:
            send(total.at[spot], total.at[spot], {"tensor": to}, name + "4", name + "4")
        yield
        got(name + "4", got2)
        spot = at(core * half, half)
        send(total.at[spot], total.at[spot], peer[1], name + "5", name + "5")
        yield
        got(name + "5", s1_b)
        yield

    def activate(c):
        in_pre[c].wait()

        @pl.loop(0, width // 32)
        def _(r):
            spot = pl.ds(pl.multiple_of(c * width + r * 32, 32), 32)
            for j in range(4):
                lanes = pl.ds(j * 256, 256)
                v = act[spot, lanes].astype(F32)
                cdf = 0.5 * (1.0 + lax.erf(v * 0.7071067811865476))
                density = jnp.exp(-0.5 * v * v) * 0.3989422804014327
                act[spot, lanes] = (v * cdf).astype(BF16)
                slope[spot, lanes] = cdf + v * density

        @pl.loop(0, 4)
        def _(j):
            act_t[at(j * 256, 256), rows(c)] = act[rows(c), at(j * 256, 256)].T

    up2, up3, up4, up5 = [], [], [], []

    def give_upstream(c):
        up0[c].wait_recv()
        up2.append(send(u.at[0, rows(c)], u.at[2, rows(c)], peer[2], "up"))
        up4.append(send(u.at[0, rows(c)], u.at[4, rows(c)], peer[8], "up"))
        send(u.at[0, rows(c)], u.at[1, rows(c)], peer[1], "up", "up1")

    def pass_upstream(c):
        up2[c].wait_recv()
        up3.append(send(u.at[2, rows(c)], u.at[3, rows(c)], peer[6], "up"))
        up4[c].wait_recv()
        up5.append(send(u.at[4, rows(c)], u.at[5, rows(c)], peer[24], "up"))

    x2, x4 = [], []
    parts = [pl.ds(n * 64, 64) for n in range(4)]

    def give_inputs(n):
        x2.append(send(xt.at[0, parts[n]], xt.at[2, parts[n]], peer[2], "in"))
        x4.append(send(xt.at[0, parts[n]], xt.at[4, parts[n]], peer[8], "in"))
        send(xt.at[0, parts[n]], xt.at[1, parts[n]], peer[1], "in", "in")

    def pass_inputs(n):
        x2[n].wait_recv()
        send(xt.at[2, parts[n]], xt.at[3, parts[n]], peer[6], "in", "in")
        x4[n].wait_recv()
        send(xt.at[4, parts[n]], xt.at[5, parts[n]], peer[24], "in", "in")

    def block_terms(c):
        for group in (up3, up5):
            group[c].wait_recv()
        left = jnp.concatenate([u[k, rows(c), :] for k in range(6)], axis=1)

        @pl.loop(0, 4)
        def _(j):
            block = at(j * 256, 256)
            right = jnp.concatenate([w2[k, block, :] for k in range(6)], axis=1)
            ga[rows(c), block] = nt(left, right)

    def second_terms(first, last):
        @pl.loop(first, last)
        def _(k):
            value = nn(act_t[...], u[k]).astype(BF16)
            for i in range(4):
                sg[i, k] = value[i * 256 : (i + 1) * 256]

    in_x.wait()
    for n in range(2):
        xt[0, pl.ds(n * 128, 128), :] = xin[:, pl.ds(n * 128, 128)].T
    give_inputs(0)
    give_inputs(1)
    activate(0)
    activate(1)
    activate(2)
    in_hand.wait()
    in_r2.wait_recv()
    pg_ar[0][...] = nt(hand[...], r2[...])
    pg = summing_all(pg_ar, u.at[6], "pg", ship=True)
    next(pg)
    give_upstream(0)
    activate(3)
    next(pg)
    pass_inputs(0)
    for copy in in_small:
        copy.wait()
    pa_ar[0][pl.ds(0, 256), :] = nn(l1[...].T, xt[0])
    pa_ar[0][pl.ds(256, 256), :] = nn(w2[6].T, act_t[...])
    pa = summing(pa_ar, paf, "pa")
    next(pa)
    give_upstream(1)
    pass_inputs(1)
    pass_upstream(0)
    give_upstream(2)
    give_upstream(3)
    pass_upstream(1)
    second_terms(0, 1)
    give_inputs(2)
    pass_upstream(2)
    next(pg)
    got("up1", u.at[1])
    second_terms(1, 2)
    pass_upstream(3)
    next(pg)
    next(pa)
    give_inputs(3)
    loaded("w2", w2.at[pl.ds(0, 6)])
    block_terms(0)
    block_terms(1)
    pass_inputs(2)
    second_terms(2, 3)
    block_terms(2)
    second_terms(4, 5)
    block_terms(3)
    next(pg)
    second_terms(3, 4)
    pass_inputs(3)
    second_terms(5, 6)
    next(pg)
    next(pa)

    loaded("w1", w1)
    far2, far4 = [], []

    def hidden(c):
        @pl.loop(0, 2)
        def _(j):
            block = at(j * 512, 512)
            grad = ga[rows(c), block] + nt(u[6, rows(c), :], w2[6, block, :])
            hid[rows(c), block] = (grad * slope[rows(c), block]).astype(BF16)

    def both(h):
        return pl.ds(h * 2 * width, 2 * width)

    def far_terms(c):
        left = hid[rows(c), :]
        p_out[3, rows(c), :] = nt(left, w1[3]).astype(BF16)
        p_out[4, rows(c), :] = nt(left, w1[5]).astype(BF16)

    def far_sends(c):
        far2.append(send(p_out.at[3, rows(c)], p_in.at[3, rows(c)], peer[6], "p"))
        far4.append(send(p_out.at[4, rows(c)], p_in.at[4, rows(c)], peer[24], "p"))

    def near_terms(h):
        left = hid[both(h), :]
        p_out[0, both(h), :] = nt(left, w1[1]).astype(BF16)
        for c in (2 * h, 2 * h + 1):
            send(p_out.at[0, rows(c)], p_in.at[0, rows(c)], peer[1], "p", "p")
        ga[both(h), pl.ds(256, 256)] = nt(left, w1[2])
        ga[both(h), pl.ds(512, 256)] = nt(left, w1[4])
        ga[both(h), pl.ds(0, 256)] = nt(left, w1[0])

    def merge(c):
        for n, far, mask in ((1, far2, 2), (2, far4, 8)):
            far[c].wait_recv()
            own = ga[rows(c), pl.ds(256 * n, 256)]
            p_out[n, rows(c), :] = (own + p_in[n + 2, rows(c), :].astype(F32)).astype(BF16)
            send(p_out.at[n, rows(c)], p_in.at[n, rows(c)], peer[mask], "p", "p")

    def first_terms(first, last):
        @pl.loop(first, last)
        def _(k):
            for i in range(4):
                block = pl.ds(i * 256, 256)
                fg[i, k] = nn(xt[k], hid[:, block]).astype(BF16)

    hidden(0)
    far_terms(0)
    far_sends(0)
    hidden(1)
    far_terms(1)
    far_sends(1)
    hidden(2)
    hidden(3)
    br_ar[0][...] = nt(hid[...], w1[6])
    back = summing_all(br_ar, br, "br")
    next(back)
    far_terms(2)
    next(back)
    far_sends(2)
    next(pa)
    far_terms(3)
    far_sends(3)
    near_terms(0)
    near_terms(1)
    got("in", xt.at[pl.ds(0, 3)])
    merge(0)
    merge(1)
    first_terms(0, 1)
    next(back)
    first_terms(1, 2)
    merge(2)
    first_terms(2, 3)
    merge(3)
    next(pa)
    first_terms(3, 6)
    l2g[...] = nn(act_t[...], u[6]).astype(BF16)
    next(back)
    next(pa)
    got("p", p_in.at[pl.ds(0, 3)])
    for c in range(CHUNKS):
        value = ga[rows(c), pl.ds(0, 256)]
        for n in range(3):
            value = value + p_in[n, rows(c), :].astype(F32)
        ga[rows(c), pl.ds(0, 256)] = value
    next(back)
    l1g[...] = nn(xt[0], br[...]).astype(BF16)
    ig[...] = (ga[:, pl.ds(0, 256)] + nt(br[...], l1[...])).astype(BF16)
    next(pa)
    r1g[...] = nn(paf[pl.ds(0, 256), :], hid[...]).astype(BF16)
    r2g[...] = nn(paf[pl.ds(256, 256), :], u[0]).astype(BF16)
    sent("r2", r2)
    sent("hand", hand)
    sent("up", u.at[pl.ds(0, 5)])
    sent("in", xt.at[pl.ds(0, 5)])
    sent("p", p_out)
    for name, (part, got1, s1, s1_b, got2, *_) in (("pg", pg_ar), ("br", br_ar)):
        sent(name + "1", got1)
        sent(name + "2", got2)
        if name == "pg":
            sent("pg3", pg_ar[5])
        sent(name + "4", got2)
        sent(name + "5", s1_b)
    part, got1, s1, s1_b, got2, s2, got3, _ = pa_ar
    sent("pa1", got1)
    sent("pa2", got2)
    sent("pa3", got3)
    sent("pa4", s1_b.at[pl.ds(0, 48)])
    sent("pa5", got2)
    sent("pa6", s1_b)


def write_out(*refs):
    count = len(refs) // 2
    sems = refs[-1]
    copies = [pltpu.make_async_copy(refs[n], refs[count + n], sems.at[n]) for n in range(count)]
    for copy in copies:
        copy.start()
    for copy in copies:
        copy.wait()


def sum_buffers(size, lanes):
    return (
        pltpu.VMEM((size, lanes), F32),
        pltpu.VMEM((size // 2, lanes), F32),
        pltpu.VMEM((size // 2, lanes), F32),
        pltpu.VMEM((size // 2, lanes), BF16),
        pltpu.VMEM((3, size // 8, lanes), BF16),
        pltpu.VMEM((size // 8, lanes), F32),
        pltpu.VMEM((3, size // 32, lanes), F32),
        pltpu.VMEM((size // 32, lanes), BF16),
    )


def wide_buffers(size, lanes):
    return (
        pltpu.VMEM((size, lanes), F32),
        pltpu.VMEM((size // 2, lanes), F32),
        pltpu.VMEM((size // 2, lanes), F32),
        pltpu.VMEM((size // 2, lanes), BF16),
        pltpu.VMEM((15, size // 32, lanes), BF16),
        pltpu.VMEM((size // 32, lanes), BF16),
    )


def body(*args):
    args = [a[0] for a in args]
    x, pre, _, fb, _, l1, r1, l2, r2 = args
    t, b = x.shape
    h = pre.shape[1]
    k = fb.shape[1]
    outs = [x, fb, fb, l1, r1, l2, r2]
    vm = pltpu.VMEM
    scratch = [
        vm((t, b), BF16), vm((t, b), BF16), vm((k, b, t), BF16), vm((k + 1, t, b), BF16),
        vm((t, h), BF16), vm((h, t), BF16), vm((t, h), F32), vm((t, h), F32),
        vm((k + 1, b, h), BF16), vm((k + 1, h, b), BF16), vm((t, h), BF16), vm((b, b), BF16),
        vm((b, b), BF16), vm((2 * b, t), BF16), vm((t, b), BF16), vm((5, t, b), BF16),
        vm((5, t, b), BF16), wide_buffers(t, b), sum_buffers(2 * b, t),
        wide_buffers(t, b),
        pltpu.SemaphoreType.DMA((20,)), pltpu.SemaphoreType.DMA((55,)),
        pltpu.SemaphoreType.DMA((11,)),
    ]
    results = pl.pallas_call(
        kernel,
        out_shape=[pltpu.VMEM(o.shape, o.dtype) for o in outs],
        in_specs=[pl.BlockSpec(memory_space=pl.ANY)] * 9,
        out_specs=[pl.BlockSpec(memory_space=pltpu.VMEM)] * 7,
        scratch_shapes=scratch,
        compiler_params=pltpu.CompilerParams(
            collective_id=0, has_side_effects=True, vmem_limit_bytes=50 * 1024 * 1024
        ),
    )(*args)
    results = pl.pallas_call(
        write_out,
        out_shape=[jax.ShapeDtypeStruct(o.shape, o.dtype) for o in outs],
        in_specs=[pl.BlockSpec(memory_space=pltpu.VMEM)] * 7,
        out_specs=[pl.BlockSpec(memory_space=pl.ANY)] * 7,
        scratch_shapes=[pltpu.SemaphoreType.DMA((7,))],
        compiler_params=pltpu.CompilerParams(vmem_limit_bytes=2 * 1024 * 1024),
    )(*[pltpu.with_memory_space_constraint(r, pltpu.VMEM) for r in results])
    return tuple(r[None] for r in results)


def solution(mesh):
    three = P("section", None, "tensor")
    rows = P("section", "tensor", None)
    blocks = P("section", "tensor", None, None, None)
    return jax.shard_map(
        body,
        mesh=mesh,
        in_specs=(three, three, three, blocks, blocks, rows, three, rows, three),
        out_specs=(three, blocks, blocks, rows, three, rows, three),
        check_vma=False,
    )
```
